32 devices in a mesh: freq: 8 (over z, x), unk: 4 (over y, core).
Axes of the slice: x: 2, y: 2, z: 4, core: 2. Of those that a mesh axis runs over, the one named last changes fastest.
Arguments:
- time_samples: bfloat16 [16, 32, 2048], P(None, 'freq', 'unk'), may hold values from -3 to 3
- inverse_offset: bfloat16 [2, 8, 2048, 512], P(None, 'freq', 'unk'), may hold values from -0.09375 to 0.09375
- coupling_near: bfloat16 [2, 8, 2048, 512], P(None, 'freq', 'unk'), may hold values from -0.125 to 0.125
- coupling_far: bfloat16 [2, 8, 2048, 512], P(None, 'freq', 'unk'), may hold values from -0.09375 to 0.09375
Outputs:
- solution: bfloat16 [2, 8, 32, 2048], P(None, 'freq', None, 'unk')
The draws below stay inside these ranges and needn't reach their ends.
All inputs are finite; a program needn't handle non-finite values.
Results may differ from the reference program's by a relative error of at most 0.017.
Values may be sent and summed in bfloat16 or wider, within the bound.
A program may use at most 64 MiB of HBM per device.

```python
import math
import jax
import jax.numpy as jnp
from jax import lax

ROWS = 512
FREQS = 8
TIMES = 16
LOADS = 32
UNKNOWNS = 2048


def shard_levels(stream_key, dims, cuts, low, top_value):
    def one(axis_at, parts):
        draws = jax.random.uniform(jax.random.fold_in(jax.random.fold_in(stream_key, 6), axis_at), (parts,), jnp.float32, low / len(cuts), top_value / len(cuts))
        return jnp.repeat(jnp.exp(draws), dims[axis_at] // parts).reshape((-1,) + (1,) * (len(dims) - axis_at - 1))

    level = one(*cuts[0])
    for cut in cuts[1:]:
        level = level * one(*cut)
    return level


def normal_values(stream_key, extent, width, bound, pieces=(), kind=jnp.bfloat16):
    values = width * jax.random.normal(stream_key, extent, jnp.float32)
    if pieces:
        values = values * shard_levels(stream_key, extent, pieces, -0.22, 0.18)
    return jnp.clip(values, -bound, bound).astype(kind)


def setup_inputs(seed: int = 0) -> dict:
    seeds = jax.random.split(jax.random.key(seed), 5)
    time_samples = normal_values(seeds[0], (TIMES, LOADS, UNKNOWNS), 0.5, 3.0, ((1, 8), (2, 4)))
    inverse_offset = normal_values(seeds[1], (2, FREQS, UNKNOWNS, ROWS), (ROWS * 8) ** -0.5, 0.09375, ((1, 8), (2, 4)))
    coupling_near = normal_values(seeds[2], (2, FREQS, UNKNOWNS, ROWS), (ROWS * 4) ** -0.5, 0.125, ((1, 8), (2, 4)))
    coupling_far = normal_values(seeds[3], (2, FREQS, UNKNOWNS, ROWS), (ROWS * 8) ** -0.5, 0.09375, ((1, 8), (2, 4)))
    return {"time_samples": time_samples, "inverse_offset": inverse_offset, "coupling_near": coupling_near, "coupling_far": coupling_far}


def complex_product(factor_one, factor_two):
    first_real = factor_one[0].astype(jnp.float32)
    first_imag = factor_one[1].astype(jnp.float32)
    second_real = factor_two[0].astype(jnp.float32)
    second_imag = factor_two[1].astype(jnp.float32)
    highest = lax.Precision.HIGHEST
    real_part = jnp.einsum('fmk,fkn->fmn', first_real, second_real, precision=highest) - jnp.einsum('fmk,fkn->fmn', first_imag, second_imag, precision=highest)
    imag_part = jnp.einsum('fmk,fkn->fmn', first_real, second_imag, precision=highest) + jnp.einsum('fmk,fkn->fmn', first_imag, second_real, precision=highest)
    return jnp.stack([real_part, imag_part])

def transform_table(time_count, freq_count):
    moment = jnp.arange(time_count, dtype=jnp.int32)
    harmonic = jnp.arange(freq_count, dtype=jnp.int32)
    phase_angle = (harmonic[:, None] * moment[None, :] % time_count).astype(jnp.float32) * (2.0 * math.pi / time_count)
    damping = jnp.power(0.5, moment.astype(jnp.float32) / time_count) / math.sqrt(time_count)
    return jnp.stack([damping * jnp.cos(phase_angle), -damping * jnp.sin(phase_angle)])

def reference(time_samples, inverse_offset, coupling_near, coupling_far):
    weights_table = transform_table(TIMES, FREQS)
    spectra = jnp.einsum('ckt,tln->ckln', weights_table, time_samples.astype(jnp.float32), precision=lax.Precision.HIGHEST).astype(jnp.bfloat16)
    blank_block = jnp.zeros((2, FREQS, LOADS, ROWS), jnp.bfloat16)
    previous = blank_block
    before_previous = blank_block
    solved = []
    for block_index in range(UNKNOWNS // ROWS):
        rows_slice = slice(block_index * ROWS, (block_index + 1) * ROWS)
        offset_block = inverse_offset[:, :, rows_slice, :]
        near_block = coupling_near[:, :, rows_slice, :]
        far_block = coupling_far[:, :, rows_slice, :]
        near_reduced = (near_block.astype(jnp.float32) + complex_product(near_block, offset_block)).astype(jnp.bfloat16)
        far_reduced = (far_block.astype(jnp.float32) + complex_product(far_block, offset_block)).astype(jnp.bfloat16)
        spectra_block = spectra[:, :, :, rows_slice]
        driven = spectra_block.astype(jnp.float32) + complex_product(spectra_block, offset_block)
        fresh_block = (driven - complex_product(previous, near_reduced) - complex_product(before_previous, far_reduced)).astype(jnp.bfloat16)
        solved.append(fresh_block)
        before_previous = previous
        previous = fresh_block
    return jnp.concatenate(solved, axis=3)
```

```python
import functools
import math

import jax
import jax.numpy as jnp
import numpy as np
from jax import lax
from jax.experimental import pallas as pl
from jax.experimental.pallas import tpu as pltpu
from jax.sharding import PartitionSpec as P

MESH = pl.DeviceIdType.MESH


def transform_matrix(times, freqs, loads):
    moment = np.arange(times)
    angle = (np.arange(freqs)[:, None] * moment[None, :] % times) * (2.0 * math.pi / times)
    damping = np.power(0.5, moment / times) / math.sqrt(times)
    table = np.stack([damping * np.cos(angle), -damping * np.sin(angle)], axis=1)
    full = np.einsum("kct,lm->kcltm", table, np.eye(loads)).astype(np.float32)
    full = full.reshape(freqs * 2 * loads, times * loads)
    high = full.astype(jnp.bfloat16)
    rest = (full - high.astype(np.float32)).astype(jnp.bfloat16)
    return np.concatenate([high, rest], axis=1)


def dot(left, right):
    return jnp.dot(left, right, preferred_element_type=jnp.float32)


def widened(value):
    half = value.shape[0] // 2
    real, imag = value[:half], value[half:]
    return jnp.concatenate(
        [jnp.concatenate([real, -imag], axis=1), jnp.concatenate([imag, real], axis=1)], axis=0
    )


def kernel(
    n_freq, n_unk, chunk,
    ts_hbm, w_hbm, o_hbm, c_hbm, f_hbm, out_ref,
    ts, w, o, c, f, near, far, sp, rb, xb, xin, acc,
    load_sem, send_sem, recv_sem, xsend_sem, xrecv_sem,
):
    me = lax.axis_index("freq")
    pos = lax.axis_index("unk")
    loads = ts.shape[1]
    rows = o.shape[1]

    copies = [
        pltpu.make_async_copy(src, dst, load_sem.at[i])
        for i, (src, dst) in enumerate(
            [(ts_hbm, ts), (w_hbm, w), (o_hbm.at[:, 0], o), (c_hbm.at[:, 0], c), (f_hbm.at[:, 0], f)]
        )
    ]
    for copy in copies:
        copy.start()

    barrier = pltpu.get_barrier_semaphore()
    for d in range(1, n_freq):
        pl.semaphore_signal(
            barrier, inc=1, device_id={"freq": lax.rem(me + d, n_freq)}, device_id_type=MESH
        )
    for d in (1, 2):
        @pl.when(pos + d < n_unk)
        def _():
            pl.semaphore_signal(barrier, inc=1, device_id={"unk": pos + d}, device_id_type=MESH)

        @pl.when(pos >= d)
        def _():
            pl.semaphore_signal(barrier, inc=1, device_id={"unk": pos - d}, device_id_type=MESH)

    copies[0].wait()
    copies[1].wait()
    samples = ts[...].astype(jnp.float32).reshape(-1, rows).astype(jnp.bfloat16)
    spectra = dot(w[...], jnp.concatenate([samples, samples], axis=0))
    sp[...] = spectra.reshape(sp.shape).astype(jnp.bfloat16)

    def reduce_block(src, dst):
        def part(i):
            at = pl.ds(pl.multiple_of(i * chunk, chunk), chunk)
            real, imag = src[0, at, :], src[1, at, :]
            weights = o[...].reshape(2 * rows, rows)
            new_real = dot(jnp.concatenate([real, -imag], axis=1), weights)
            dst[0, at, :] = (real.astype(jnp.float32) + new_real).astype(jnp.bfloat16)
            new_imag = dot(jnp.concatenate([imag, real], axis=1), weights)
            dst[1, at, :] = (imag.astype(jnp.float32) + new_imag).astype(jnp.bfloat16)

        pl.loop(0, rows // chunk)(part)

    copies[2].wait()
    copies[3].wait()
    copies[4].wait()

    pl.semaphore_wait(
        barrier,
        n_freq - 1
        + sum(
            (pos + d < n_unk).astype(jnp.int32) + (pos >= d).astype(jnp.int32) for d in (1, 2)
        ),
    )

    sends = []
    for d in range(1, n_freq):
        target = lax.rem(me + d, n_freq)
        send = pltpu.make_async_remote_copy(
            src_ref=sp.at[target], dst_ref=rb.at[me],
            send_sem=send_sem.at[d], recv_sem=recv_sem.at[me],
            device_id={"freq": target}, device_id_type=MESH,
        )
        send.start()
        sends.append(send)
    rb[me] = sp[me]

    @pl.when(pos >= 1)
    def _():
        reduce_block(c, near)

    @pl.when(pos >= 2)
    def _():
        reduce_block(f, far)

    for d in range(1, n_freq):
        source = lax.rem(me + n_freq - d, n_freq)
        pltpu.make_async_remote_copy(
            src_ref=rb.at[source], dst_ref=rb.at[source],
            send_sem=send_sem.at[d], recv_sem=recv_sem.at[source],
            device_id={"freq": source}, device_id_type=MESH,
        ).wait_recv()

    got = rb[...].astype(jnp.float32)
    got = jnp.concatenate(
        [got[:, :loads].reshape(-1, rows), got[:, loads:].reshape(-1, rows)], axis=0
    )
    driven = got + dot(widened(got.astype(jnp.bfloat16)), o[...].reshape(2 * rows, rows))
    acc[...] = driven

    def hop(slot, step):
        return pltpu.make_async_remote_copy(
            src_ref=xb, dst_ref=xin.at[slot],
            send_sem=xsend_sem.at[slot], recv_sem=xrecv_sem.at[slot],
            device_id={"unk": lax.rem(pos + step, n_unk)}, device_id_type=MESH,
        )

    @pl.when(pos >= 2)
    def _():
        hop(1, 2).wait_recv()
        acc[...] -= dot(widened(xin[1]), far[...].reshape(2 * rows, rows))

    @pl.when(pos >= 1)
    def _():
        hop(0, 1).wait_recv()
        acc[...] -= dot(widened(xin[0]), near[...].reshape(2 * rows, rows))

    xb[...] = acc[...].astype(jnp.bfloat16)

    @pl.when(pos + 1 < n_unk)
    def _():
        hop(0, 1).start()

    @pl.when(pos + 2 < n_unk)
    def _():
        hop(1, 2).start()

    out_ref[...] = xb[...].reshape(out_ref.shape)

    for send in sends:
        send.wait_send()

    @pl.when(pos + 1 < n_unk)
    def _():
        hop(0, 1).wait_send()

    @pl.when(pos + 2 < n_unk)
    def _():
        hop(1, 2).wait_send()


def per_device(n_freq, n_unk, time_samples, inverse_offset, coupling_near, coupling_far):
    times, loads, rows = time_samples.shape
    freqs = inverse_offset.shape[1] * n_freq
    table = jnp.asarray(transform_matrix(times, freqs, loads))
    block = (2, rows, rows)
    wide = 2 * n_freq * loads
    bf16 = jnp.bfloat16
    return pl.pallas_call(
        functools.partial(kernel, n_freq, n_unk, min(256, rows)),
        out_shape=jax.ShapeDtypeStruct((2, 1, n_freq * loads, rows), bf16),
        in_specs=[pl.BlockSpec(memory_space=pl.ANY)] * 5,
        out_specs=pl.BlockSpec(memory_space=pltpu.VMEM),
        scratch_shapes=[
            pltpu.VMEM(time_samples.shape, bf16),
            pltpu.VMEM(table.shape, bf16),
            pltpu.VMEM(block, bf16),
            pltpu.VMEM(block, bf16),
            pltpu.VMEM(block, bf16),
            pltpu.VMEM(block, bf16),
            pltpu.VMEM(block, bf16),
            pltpu.VMEM((n_freq, 2 * loads, rows), bf16),
            pltpu.VMEM((n_freq, 2 * loads, rows), bf16),
            pltpu.VMEM((wide, rows), bf16),
            pltpu.VMEM((2, wide, rows), bf16),
            pltpu.VMEM((wide, rows), jnp.float32),
            pltpu.SemaphoreType.DMA((5,)),
            pltpu.SemaphoreType.DMA((n_freq,)),
            pltpu.SemaphoreType.DMA((n_freq,)),
            pltpu.SemaphoreType.DMA((2,)),
            pltpu.SemaphoreType.DMA((2,)),
        ],
        compiler_params=pltpu.CompilerParams(collective_id=0, has_side_effects=True),
    )(time_samples, table, inverse_offset, coupling_near, coupling_far)


def solution(mesh):
    placed = (
        P(None, "freq", "unk"),
        P(None, "freq", "unk", None),
        P(None, "freq", "unk", None),
        P(None, "freq", "unk", None),
    )
    return jax.shard_map(
        functools.partial(per_device, mesh.shape["freq"], mesh.shape["unk"]),
        mesh=mesh,
        in_specs=placed,
        out_specs=P(None, "freq", None, "unk"),
        check_vma=False,
    )
```

```python
import functools
import math

import jax
import jax.numpy as jnp
import numpy as np
from jax import lax
from jax.experimental import pallas as pl
from jax.experimental.pallas import tpu as pltpu
from jax.sharding import PartitionSpec as P

MESH = pl.DeviceIdType.MESH


def transform_matrix(times, freqs, loads):
    moment = np.arange(times)
    angle = (np.arange(freqs)[:, None] * moment[None, :] % times) * (2.0 * math.pi / times)
    damping = np.power(0.5, moment / times) / math.sqrt(times)
    table = np.stack([damping * np.cos(angle), -damping * np.sin(angle)], axis=1)
    full = np.einsum("kct,lm->kcltm", table, np.eye(loads)).astype(np.float32)
    full = full.reshape(freqs * 2 * loads, times * loads)
    high = full.astype(jnp.bfloat16)
    rest = (full - high.astype(np.float32)).astype(jnp.bfloat16)
    return np.concatenate([high, rest], axis=1)


def dot(left, right):
    return jnp.dot(left, right, preferred_element_type=jnp.float32)


def widened(value):
    half = value.shape[0] // 2
    real, imag = value[:half], value[half:]
    return jnp.concatenate(
        [jnp.concatenate([real, -imag], axis=1), jnp.concatenate([imag, real], axis=1)], axis=0
    )


def kernel(
    n_freq, n_unk, chunk,
    ts_hbm, w_hbm, o_hbm, c_hbm, f_hbm, out_ref,
    ts, w, o, c, f, near, far, sp, rb, xb, xin, acc,
    load_sem, send_sem, recv_sem, xsend_sem, xrecv_sem,
):
    me = lax.axis_index("freq")
    pos = lax.axis_index("unk")
    loads = ts.shape[1]
    rows = o.shape[1]

    copies = [
        pltpu.make_async_copy(src, dst, load_sem.at[i])
        for i, (src, dst) in enumerate(
            [(ts_hbm, ts), (w_hbm, w), (o_hbm.at[:, 0], o), (c_hbm.at[:, 0], c), (f_hbm.at[:, 0], f)]
        )
    ]
    for copy in copies:
        copy.start()

    barrier = pltpu.get_barrier_semaphore()
    for d in range(1, n_freq):
        pl.semaphore_signal(
            barrier, inc=1, device_id={"freq": lax.rem(me + d, n_freq)}, device_id_type=MESH
        )
    for d in (1, 2):
        @pl.when(pos + d < n_unk)
        def _():
            pl.semaphore_signal(barrier, inc=1, device_id={"unk": pos + d}, device_id_type=MESH)

        @pl.when(pos >= d)
        def _():
            pl.semaphore_signal(barrier, inc=1, device_id={"unk": pos - d}, device_id_type=MESH)

    copies[0].wait()
    copies[1].wait()
    samples = ts[...].astype(jnp.float32).reshape(-1, rows).astype(jnp.bfloat16)
    spectra = dot(w[...], jnp.concatenate([samples, samples], axis=0))
    sp[...] = spectra.reshape(sp.shape).astype(jnp.bfloat16)

    def reduce_block(src, dst):
        def part(i):
            at = pl.ds(pl.multiple_of(i * chunk, chunk), chunk)
            real, imag = src[0, at, :], src[1, at, :]
            weights = o[...].reshape(2 * rows, rows)
            new_real = dot(jnp.concatenate([real, -imag], axis=1), weights)
            dst[0, at, :] = (real.astype(jnp.float32) + new_real).astype(jnp.bfloat16)
            new_imag = dot(jnp.concatenate([imag, real], axis=1), weights)
            dst[1, at, :] = (imag.astype(jnp.float32) + new_imag).astype(jnp.bfloat16)

        pl.loop(0, rows // chunk)(part)

    pl.semaphore_wait(
        barrier,
        n_freq - 1
        + sum(
            (pos + d < n_unk).astype(jnp.int32) + (pos >= d).astype(jnp.int32) for d in (1, 2)
        ),
    )

    sends = []
    upper = (me * 2) // n_freq
    for d in range(1, n_freq):
        rising = (d - 1) + (d - 1 >= me).astype(jnp.int32)
        falling = (n_freq - d) - (n_freq - d <= me).astype(jnp.int32)
        target = upper * rising + (1 - upper) * falling
        send = pltpu.make_async_remote_copy(
            src_ref=sp.at[target], dst_ref=rb.at[me],
            send_sem=send_sem.at[d], recv_sem=recv_sem.at[me],
            device_id={"freq": target}, device_id_type=MESH,
        )
        send.start()
        sends.append(send)
    rb[me] = sp[me]

    copies[2].wait()
    copies[3].wait()
    copies[4].wait()

    @pl.when(pos >= 1)
    def _():
        reduce_block(c, near)

    @pl.when(pos >= 2)
    def _():
        reduce_block(f, far)

    for d in range(1, n_freq):
        source = lax.rem(me + n_freq - d, n_freq)
        pltpu.make_async_remote_copy(
            src_ref=rb.at[source], dst_ref=rb.at[source],
            send_sem=send_sem.at[d], recv_sem=recv_sem.at[source],
            device_id={"freq": source}, device_id_type=MESH,
        ).wait_recv()

    got = rb[...].astype(jnp.float32)
    got = jnp.concatenate(
        [got[:, :loads].reshape(-1, rows), got[:, loads:].reshape(-1, rows)], axis=0
    )
    driven = got + dot(widened(got.astype(jnp.bfloat16)), o[...].reshape(2 * rows, rows))
    acc[...] = driven

    def hop(slot, step):
        return pltpu.make_async_remote_copy(
            src_ref=xb, dst_ref=xin.at[slot],
            send_sem=xsend_sem.at[slot], recv_sem=xrecv_sem.at[slot],
            device_id={"unk": lax.rem(pos + step, n_unk)}, device_id_type=MESH,
        )

    @pl.when(pos >= 2)
    def _():
        hop(1, 2).wait_recv()
        acc[...] -= dot(widened(xin[1]), far[...].reshape(2 * rows, rows))

    @pl.when(pos >= 1)
    def _():
        hop(0, 1).wait_recv()
        acc[...] -= dot(widened(xin[0]), near[...].reshape(2 * rows, rows))

    xb[...] = acc[...].astype(jnp.bfloat16)

    @pl.when(pos + 1 < n_unk)
    def _():
        hop(0, 1).start()

    @pl.when(pos + 2 < n_unk)
    def _():
        hop(1, 2).start()

    out_ref[...] = xb[...].reshape(out_ref.shape)

    for send in sends:
        send.wait_send()

    @pl.when(pos + 1 < n_unk)
    def _():
        hop(0, 1).wait_send()

    @pl.when(pos + 2 < n_unk)
    def _():
        hop(1, 2).wait_send()


def per_device(n_freq, n_unk, time_samples, inverse_offset, coupling_near, coupling_far):
    times, loads, rows = time_samples.shape
    freqs = inverse_offset.shape[1] * n_freq
    table = jnp.asarray(transform_matrix(times, freqs, loads))
    block = (2, rows, rows)
    wide = 2 * n_freq * loads
    bf16 = jnp.bfloat16
    return pl.pallas_call(
        functools.partial(kernel, n_freq, n_unk, min(256, rows)),
        out_shape=pltpu.VMEM((2, 1, n_freq * loads, rows), bf16),
        in_specs=[pl.BlockSpec(memory_space=pl.ANY)] * 5,
        out_specs=pl.BlockSpec(memory_space=pltpu.VMEM),
        scratch_shapes=[
            pltpu.VMEM(time_samples.shape, bf16),
            pltpu.VMEM(table.shape, bf16),
            pltpu.VMEM(block, bf16),
            pltpu.VMEM(block, bf16),
            pltpu.VMEM(block, bf16),
            pltpu.VMEM(block, bf16),
            pltpu.VMEM(block, bf16),
            pltpu.VMEM((n_freq, 2 * loads, rows), bf16),
            pltpu.VMEM((n_freq, 2 * loads, rows), bf16),
            pltpu.VMEM((wide, rows), bf16),
            pltpu.VMEM((2, wide, rows), bf16),
            pltpu.VMEM((wide, rows), jnp.float32),
            pltpu.SemaphoreType.DMA((5,)),
            pltpu.SemaphoreType.DMA((n_freq,)),
            pltpu.SemaphoreType.DMA((n_freq,)),
            pltpu.SemaphoreType.DMA((2,)),
            pltpu.SemaphoreType.DMA((2,)),
        ],
        compiler_params=pltpu.CompilerParams(collective_id=0, has_side_effects=True),
    )(time_samples, table, inverse_offset, coupling_near, coupling_far)


def solution(mesh):
    placed = (
        P(None, "freq", "unk"),
        P(None, "freq", "unk", None),
        P(None, "freq", "unk", None),
        P(None, "freq", "unk", None),
    )
    return jax.shard_map(
        functools.partial(per_device, mesh.shape["freq"], mesh.shape["unk"]),
        mesh=mesh,
        in_specs=placed,
        out_specs=P(None, "freq", None, "unk"),
        check_vma=False,
    )
```

```python
import functools
import math

import jax
import jax.numpy as jnp
import numpy as np
from jax import lax
from jax.experimental import pallas as pl
from jax.experimental.pallas import tpu as pltpu
from jax.sharding import PartitionSpec as P

MESH = pl.DeviceIdType.MESH


def transform_matrix(times, freqs, loads):
    moment = np.arange(times)
    angle = (np.arange(freqs)[:, None] * moment[None, :] % times) * (2.0 * math.pi / times)
    damping = np.power(0.5, moment / times) / math.sqrt(times)
    table = np.stack([damping * np.cos(angle), -damping * np.sin(angle)], axis=1)
    full = np.einsum("kct,lm->kcltm", table, np.eye(loads)).astype(np.float32)
    full = full.reshape(freqs * 2 * loads, times * loads)
    high = full.astype(jnp.bfloat16)
    rest = (full - high.astype(np.float32)).astype(jnp.bfloat16)
    return np.concatenate([high, rest], axis=1)


def dot(left, right):
    return jnp.dot(left, right, preferred_element_type=jnp.float32)


def widened(value):
    half = value.shape[0] // 2
    real, imag = value[:half], value[half:]
    return jnp.concatenate(
        [jnp.concatenate([real, -imag], axis=1), jnp.concatenate([imag, real], axis=1)], axis=0
    )


def kernel(
    n_freq, n_unk, chunk,
    ts_hbm, w_hbm, o_hbm, c_hbm, f_hbm, out_ref,
    ts, w, o, c, f, near, far, sp, rb, xb, xin, acc, first_o, first_rb,
    load_sem, send_sem, recv_sem, xsend_sem, xrecv_sem, first_send_sem, first_recv_sem, share_sem,
):
    me = lax.axis_index("freq")
    pos = lax.axis_index("unk")
    loads = ts.shape[1]
    rows = o.shape[1]

    copies = [
        pltpu.make_async_copy(src, dst, load_sem.at[i])
        for i, (src, dst) in enumerate(
            [(ts_hbm, ts), (w_hbm, w), (o_hbm.at[:, 0], o), (c_hbm.at[:, 0], c), (f_hbm.at[:, 0], f)]
        )
    ]
    for copy in copies:
        copy.start()

    barrier = pltpu.get_barrier_semaphore()
    for d in range(1, n_freq):
        pl.semaphore_signal(
            barrier, inc=1, device_id={"freq": lax.rem(me + d, n_freq)}, device_id_type=MESH
        )
    for d in (1, 2):
        @pl.when(pos + d < n_unk)
        def _():
            pl.semaphore_signal(barrier, inc=1, device_id={"unk": pos + d}, device_id_type=MESH)

        @pl.when(pos >= d)
        def _():
            pl.semaphore_signal(barrier, inc=1, device_id={"unk": pos - d}, device_id_type=MESH)

    @pl.when(pos == 1)
    def _():
        for d in range(1, n_freq):
            pl.semaphore_signal(
                barrier, inc=1,
                device_id={"freq": lax.rem(me + d, n_freq), "unk": 0}, device_id_type=MESH,
            )

    copies[0].wait()
    copies[1].wait()
    samples = ts[...].astype(jnp.float32).reshape(-1, rows).astype(jnp.bfloat16)
    spectra = dot(w[...], jnp.concatenate([samples, samples], axis=0))
    sp[...] = spectra.reshape(sp.shape).astype(jnp.bfloat16)

    def reduce_block(src, dst):
        def part(i):
            at = pl.ds(pl.multiple_of(i * chunk, chunk), chunk)
            real, imag = src[0, at, :], src[1, at, :]
            weights = o[...].reshape(2 * rows, rows)
            new_real = dot(jnp.concatenate([real, -imag], axis=1), weights)
            dst[0, at, :] = (real.astype(jnp.float32) + new_real).astype(jnp.bfloat16)
            new_imag = dot(jnp.concatenate([imag, real], axis=1), weights)
            dst[1, at, :] = (imag.astype(jnp.float32) + new_imag).astype(jnp.bfloat16)

        pl.loop(0, rows // chunk)(part)

    pl.semaphore_wait(
        barrier,
        (n_freq - 1) * (1 + (pos == 0).astype(jnp.int32))
        + sum(
            (pos + d < n_unk).astype(jnp.int32) + (pos >= d).astype(jnp.int32) for d in (1, 2)
        ),
    )

    def share_offset():
        return pltpu.make_async_remote_copy(
            src_ref=o_hbm.at[:, 0], dst_ref=first_o,
            send_sem=share_sem.at[0], recv_sem=share_sem.at[1],
            device_id={"unk": 1}, device_id_type=MESH,
        )

    def share_spectra(target, source, at):
        return pltpu.make_async_remote_copy(
            src_ref=sp.at[target], dst_ref=first_rb.at[source],
            send_sem=first_send_sem.at[at], recv_sem=first_recv_sem.at[source],
            device_id={"freq": target, "unk": 1}, device_id_type=MESH,
        )

    sends = []
    shares = []
    upper = (me * 2) // n_freq
    for d in range(1, n_freq):
        rising = (d - 1) + (d - 1 >= me).astype(jnp.int32)
        falling = (n_freq - d) - (n_freq - d <= me).astype(jnp.int32)
        target = upper * rising + (1 - upper) * falling
        share = share_spectra(target, me, d)
        shares.append(share)
        pl.when(pos == 0)(share.start)
        send = pltpu.make_async_remote_copy(
            src_ref=sp.at[target], dst_ref=rb.at[me],
            send_sem=send_sem.at[d], recv_sem=recv_sem.at[me],
            device_id={"freq": target}, device_id_type=MESH,
        )
        send.start()
        sends.append(send)
    shares.append(share_spectra(me, me, 0))

    @pl.when(pos == 0)
    def _():
        shares[-1].start()
        share_offset().start()

    rb[me] = sp[me]

    copies[2].wait()
    copies[3].wait()
    copies[4].wait()

    @pl.when(pos >= 1)
    def _():
        reduce_block(c, near)

    @pl.when(pos >= 2)
    def _():
        reduce_block(f, far)

    for d in range(1, n_freq):
        source = lax.rem(me + n_freq - d, n_freq)
        pltpu.make_async_remote_copy(
            src_ref=rb.at[source], dst_ref=rb.at[source],
            send_sem=send_sem.at[d], recv_sem=recv_sem.at[source],
            device_id={"freq": source}, device_id_type=MESH,
        ).wait_recv()

    odd = lax.rem(pos, 2) == 1
    ahead = lax.rem(pos + 1, n_unk)

    def to_next(slot, src, sem):
        return pltpu.make_async_remote_copy(
            src_ref=src, dst_ref=xin.at[slot],
            send_sem=xsend_sem.at[sem], recv_sem=xrecv_sem.at[slot],
            device_id={"unk": ahead}, device_id_type=MESH,
        )

    def to_second():
        return pltpu.make_async_remote_copy(
            src_ref=xb, dst_ref=xin.at[1],
            send_sem=xsend_sem.at[1], recv_sem=xrecv_sem.at[1],
            device_id={"unk": lax.rem(pos + 2, n_unk)}, device_id_type=MESH,
        )

    def drive(spectra_in, offset):
        got = spectra_in[...].astype(jnp.float32)
        got = jnp.concatenate(
            [got[:, :loads].reshape(-1, rows), got[:, loads:].reshape(-1, rows)], axis=0
        )
        return got + dot(widened(got.astype(jnp.bfloat16)), offset[...].reshape(2 * rows, rows))

    acc[...] = drive(rb, o)

    @pl.when(pos == 1)
    def _():
        for d in range(n_freq):
            source = lax.rem(me + n_freq - d, n_freq)
            share_spectra(source, source, d).wait_recv()
        share_offset().wait_recv()
        first = drive(first_rb, first_o).astype(jnp.bfloat16)
        xin[0] = first

        @pl.when(pos + 1 < n_unk)
        def _():
            to_next(1, xin.at[0], 2).start()

        acc[...] -= dot(widened(first), near[...].reshape(2 * rows, rows))


    has_next = jnp.logical_and(pos >= 1, pos + 1 < n_unk)
    has_second = jnp.logical_and(jnp.logical_and(pos >= 2, pos + 2 < n_unk), jnp.logical_not(odd))
    hands_on = jnp.logical_and(jnp.logical_and(pos >= 2, has_next), jnp.logical_not(odd))

    @pl.when(pos >= 2)
    def _():
        @pl.when(jnp.logical_not(odd))
        def _():
            to_second().wait_recv()

        @pl.when(odd)
        def _():
            to_next(1, xin.at[0], 2).wait_recv()

        acc[...] -= dot(widened(xin[1]), far[...].reshape(2 * rows, rows))

    @pl.when(pos >= 2)
    def _():
        to_next(0, xb, 0).wait_recv()

        @pl.when(hands_on)
        def _():
            to_next(1, xin.at[0], 2).start()

        acc[...] -= dot(widened(xin[0]), near[...].reshape(2 * rows, rows))

    xb[...] = acc[...].astype(jnp.bfloat16)

    @pl.when(has_next)
    def _():
        to_next(0, xb, 0).start()

    @pl.when(has_second)
    def _():
        to_second().start()

    out_ref[...] = xb[...].reshape(out_ref.shape)

    for send in sends:
        send.wait_send()

    @pl.when(pos == 0)
    def _():
        for share in shares:
            share.wait_send()
        share_offset().wait_send()

    @pl.when(jnp.logical_or(hands_on, jnp.logical_and(pos == 1, has_next)))
    def _():
        to_next(1, xin.at[0], 2).wait_send()

    @pl.when(has_next)
    def _():
        to_next(0, xb, 0).wait_send()

    @pl.when(has_second)
    def _():
        to_second().wait_send()


def per_device(n_freq, n_unk, time_samples, inverse_offset, coupling_near, coupling_far):
    times, loads, rows = time_samples.shape
    freqs = inverse_offset.shape[1] * n_freq
    table = jnp.asarray(transform_matrix(times, freqs, loads))
    block = (2, rows, rows)
    wide = 2 * n_freq * loads
    bf16 = jnp.bfloat16
    return pl.pallas_call(
        functools.partial(kernel, n_freq, n_unk, min(256, rows)),
        out_shape=pltpu.VMEM((2, 1, n_freq * loads, rows), bf16),
        in_specs=[pl.BlockSpec(memory_space=pl.ANY)] * 5,
        out_specs=pl.BlockSpec(memory_space=pltpu.VMEM),
        scratch_shapes=[
            pltpu.VMEM(time_samples.shape, bf16),
            pltpu.VMEM(table.shape, bf16),
            pltpu.VMEM(block, bf16),
            pltpu.VMEM(block, bf16),
            pltpu.VMEM(block, bf16),
            pltpu.VMEM(block, bf16),
            pltpu.VMEM(block, bf16),
            pltpu.VMEM((n_freq, 2 * loads, rows), bf16),
            pltpu.VMEM((n_freq, 2 * loads, rows), bf16),
            pltpu.VMEM((wide, rows), bf16),
            pltpu.VMEM((2, wide, rows), bf16),
            pltpu.VMEM((wide, rows), jnp.float32),
            pltpu.VMEM(block, bf16),
            pltpu.VMEM((n_freq, 2 * loads, rows), bf16),
            pltpu.SemaphoreType.DMA((5,)),
            pltpu.SemaphoreType.DMA((n_freq,)),
            pltpu.SemaphoreType.DMA((n_freq,)),
            pltpu.SemaphoreType.DMA((3,)),
            pltpu.SemaphoreType.DMA((2,)),
            pltpu.SemaphoreType.DMA((n_freq,)),
            pltpu.SemaphoreType.DMA((n_freq,)),
            pltpu.SemaphoreType.DMA((2,)),
        ],
        compiler_params=pltpu.CompilerParams(collective_id=0, has_side_effects=True),
    )(time_samples, table, inverse_offset, coupling_near, coupling_far)


def solution(mesh):
    placed = (
        P(None, "freq", "unk"),
        P(None, "freq", "unk", None),
        P(None, "freq", "unk", None),
        P(None, "freq", "unk", None),
    )
    return jax.shard_map(
        functools.partial(per_device, mesh.shape["freq"], mesh.shape["unk"]),
        mesh=mesh,
        in_specs=placed,
        out_specs=P(None, "freq", None, "unk"),
        check_vma=False,
    )
```

```python
import functools
import math

import jax
import jax.numpy as jnp
import numpy as np
from jax import lax
from jax.experimental import pallas as pl
from jax.experimental.pallas import tpu as pltpu
from jax.sharding import PartitionSpec as P

MESH = pl.DeviceIdType.MESH


def transform_matrix(times, freqs, loads):
    moment = np.arange(times)
    angle = (np.arange(freqs)[:, None] * moment[None, :] % times) * (2.0 * math.pi / times)
    damping = np.power(0.5, moment / times) / math.sqrt(times)
    table = np.stack([damping * np.cos(angle), -damping * np.sin(angle)], axis=1)
    full = np.einsum("kct,lm->kcltm", table, np.eye(loads)).astype(np.float32)
    full = full.reshape(freqs * 2 * loads, times * loads)
    high = full.astype(jnp.bfloat16)
    rest = (full - high.astype(np.float32)).astype(jnp.bfloat16)
    return np.concatenate([high, rest], axis=1)


def dot(left, right):
    return jnp.dot(left, right, preferred_element_type=jnp.float32)


def widened(value):
    half = value.shape[0] // 2
    real, imag = value[:half], value[half:]
    return jnp.concatenate(
        [jnp.concatenate([real, -imag], axis=1), jnp.concatenate([imag, real], axis=1)], axis=0
    )


def kernel(
    n_freq, n_unk, chunk,
    ts_hbm, w_hbm, o_hbm, c_hbm, f_hbm, out_ref,
    ts, w, o, c, f, near, far, sp, rb, xb, xin, acc, first_o, first_rb,
    load_sem, send_sem, recv_sem, xsend_sem, xrecv_sem, first_send_sem, first_recv_sem, share_sem,
):
    me = lax.axis_index("freq")
    pos = lax.axis_index("unk")
    loads = ts.shape[1]
    rows = o.shape[1]

    copies = [
        pltpu.make_async_copy(src, dst, load_sem.at[i])
        for i, (src, dst) in enumerate(
            [(ts_hbm, ts), (w_hbm, w), (o_hbm.at[:, 0], o), (c_hbm.at[:, 0], c), (f_hbm.at[:, 0], f)]
        )
    ]
    for copy in copies:
        copy.start()

    barrier = pltpu.get_barrier_semaphore()
    for d in range(1, n_freq):
        pl.semaphore_signal(
            barrier, inc=1, device_id={"freq": lax.rem(me + d, n_freq)}, device_id_type=MESH
        )
    for d in (1, 2):
        @pl.when(pos + d < n_unk)
        def _():
            pl.semaphore_signal(barrier, inc=1, device_id={"unk": pos + d}, device_id_type=MESH)

        @pl.when(pos >= d)
        def _():
            pl.semaphore_signal(barrier, inc=1, device_id={"unk": pos - d}, device_id_type=MESH)

    @pl.when(pos == 1)
    def _():
        for d in range(1, n_freq):
            pl.semaphore_signal(
                barrier, inc=1,
                device_id={"freq": lax.rem(me + d, n_freq), "unk": 0}, device_id_type=MESH,
            )

    copies[0].wait()
    copies[1].wait()
    samples = ts[...].astype(jnp.float32).reshape(-1, rows).astype(jnp.bfloat16)
    spectra = dot(w[...], jnp.concatenate([samples, samples], axis=0))
    sp[...] = spectra.reshape(sp.shape).astype(jnp.bfloat16)

    def reduce_block(src, dst):
        def part(i):
            at = pl.ds(pl.multiple_of(i * chunk, chunk), chunk)
            real, imag = src[0, at, :], src[1, at, :]
            weights = o[...].reshape(2 * rows, rows)
            new_real = dot(jnp.concatenate([real, -imag], axis=1), weights)
            dst[0, at, :] = (real.astype(jnp.float32) + new_real).astype(jnp.bfloat16)
            new_imag = dot(jnp.concatenate([imag, real], axis=1), weights)
            dst[1, at, :] = (imag.astype(jnp.float32) + new_imag).astype(jnp.bfloat16)

        pl.loop(0, rows // chunk)(part)

    pl.semaphore_wait(
        barrier,
        (n_freq - 1) * (1 + (pos == 0).astype(jnp.int32))
        + sum(
            (pos + d < n_unk).astype(jnp.int32) + (pos >= d).astype(jnp.int32) for d in (1, 2)
        ),
    )

    def share_offset():
        return pltpu.make_async_remote_copy(
            src_ref=o_hbm.at[:, 0], dst_ref=first_o,
            send_sem=share_sem.at[0], recv_sem=share_sem.at[1],
            device_id={"unk": 1}, device_id_type=MESH,
        )

    def share_spectra(target, source, at):
        return pltpu.make_async_remote_copy(
            src_ref=sp.at[target], dst_ref=first_rb.at[source],
            send_sem=first_send_sem.at[at], recv_sem=first_recv_sem.at[source],
            device_id={"freq": target, "unk": 1}, device_id_type=MESH,
        )

    def other(d):
        upper = (me * 2) // n_freq
        rising = (d - 1) + (d - 1 >= me).astype(jnp.int32)
        falling = (n_freq - d) - (n_freq - d <= me).astype(jnp.int32)
        return upper * rising + (1 - upper) * falling

    @pl.when(pos == 0)
    def _():
        for d in range(1, n_freq):
            share_spectra(other(d), me, d).start()
        share_spectra(me, me, 0).start()
        share_offset().start()

    sends = []
    for d in range(1, n_freq):
        target = other(d)
        send = pltpu.make_async_remote_copy(
            src_ref=sp.at[target], dst_ref=rb.at[me],
            send_sem=send_sem.at[d], recv_sem=recv_sem.at[me],
            device_id={"freq": target}, device_id_type=MESH,
        )
        send.start()
        sends.append(send)
    rb[me] = sp[me]

    copies[2].wait()
    copies[3].wait()
    copies[4].wait()

    @pl.when(pos >= 1)
    def _():
        reduce_block(c, near)

    @pl.when(pos >= 2)
    def _():
        reduce_block(f, far)

    for d in range(1, n_freq):
        source = lax.rem(me + n_freq - d, n_freq)
        pltpu.make_async_remote_copy(
            src_ref=rb.at[source], dst_ref=rb.at[source],
            send_sem=send_sem.at[d], recv_sem=recv_sem.at[source],
            device_id={"freq": source}, device_id_type=MESH,
        ).wait_recv()

    odd = lax.rem(pos, 2) == 1
    ahead = lax.rem(pos + 1, n_unk)

    def to_next(slot, src, sem):
        return pltpu.make_async_remote_copy(
            src_ref=src, dst_ref=xin.at[slot],
            send_sem=xsend_sem.at[sem], recv_sem=xrecv_sem.at[slot],
            device_id={"unk": ahead}, device_id_type=MESH,
        )

    def to_second():
        return pltpu.make_async_remote_copy(
            src_ref=xb, dst_ref=xin.at[1],
            send_sem=xsend_sem.at[1], recv_sem=xrecv_sem.at[1],
            device_id={"unk": lax.rem(pos + 2, n_unk)}, device_id_type=MESH,
        )

    def drive(spectra_in, offset):
        got = spectra_in[...].astype(jnp.float32)
        got = jnp.concatenate(
            [got[:, :loads].reshape(-1, rows), got[:, loads:].reshape(-1, rows)], axis=0
        )
        return got + dot(widened(got.astype(jnp.bfloat16)), offset[...].reshape(2 * rows, rows))

    acc[...] = drive(rb, o)

    @pl.when(pos == 1)
    def _():
        for d in range(n_freq):
            source = lax.rem(me + n_freq - d, n_freq)
            share_spectra(source, source, d).wait_recv()
        share_offset().wait_recv()
        first = drive(first_rb, first_o).astype(jnp.bfloat16)
        xin[0] = first

        @pl.when(pos + 1 < n_unk)
        def _():
            to_next(1, xin.at[0], 2).start()

        acc[...] -= dot(widened(first), near[...].reshape(2 * rows, rows))


    has_next = jnp.logical_and(pos >= 1, pos + 1 < n_unk)
    has_second = jnp.logical_and(jnp.logical_and(pos >= 2, pos + 2 < n_unk), jnp.logical_not(odd))
    hands_on = jnp.logical_and(jnp.logical_and(pos >= 2, has_next), jnp.logical_not(odd))

    @pl.when(pos >= 2)
    def _():
        @pl.when(jnp.logical_not(odd))
        def _():
            to_second().wait_recv()

        @pl.when(odd)
        def _():
            to_next(1, xin.at[0], 2).wait_recv()

        acc[...] -= dot(widened(xin[1]), far[...].reshape(2 * rows, rows))

    @pl.when(pos >= 2)
    def _():
        to_next(0, xb, 0).wait_recv()

        @pl.when(hands_on)
        def _():
            to_next(1, xin.at[0], 2).start()

        acc[...] -= dot(widened(xin[0]), near[...].reshape(2 * rows, rows))

    xb[...] = acc[...].astype(jnp.bfloat16)

    @pl.when(has_next)
    def _():
        to_next(0, xb, 0).start()

    @pl.when(has_second)
    def _():
        to_second().start()

    out_ref[...] = xb[...].reshape(out_ref.shape)

    for send in sends:
        send.wait_send()

    @pl.when(pos == 0)
    def _():
        for d in range(n_freq):
            share_spectra(me, me, d).wait_send()
        share_offset().wait_send()

    @pl.when(jnp.logical_or(hands_on, jnp.logical_and(pos == 1, has_next)))
    def _():
        to_next(1, xin.at[0], 2).wait_send()

    @pl.when(has_next)
    def _():
        to_next(0, xb, 0).wait_send()

    @pl.when(has_second)
    def _():
        to_second().wait_send()


def per_device(n_freq, n_unk, time_samples, inverse_offset, coupling_near, coupling_far):
    times, loads, rows = time_samples.shape
    freqs = inverse_offset.shape[1] * n_freq
    table = jnp.asarray(transform_matrix(times, freqs, loads))
    block = (2, rows, rows)
    wide = 2 * n_freq * loads
    bf16 = jnp.bfloat16
    return pl.pallas_call(
        functools.partial(kernel, n_freq, n_unk, min(256, rows)),
        out_shape=pltpu.VMEM((2, 1, n_freq * loads, rows), bf16),
        in_specs=[pl.BlockSpec(memory_space=pl.ANY)] * 5,
        out_specs=pl.BlockSpec(memory_space=pltpu.VMEM),
        scratch_shapes=[
            pltpu.VMEM(time_samples.shape, bf16),
            pltpu.VMEM(table.shape, bf16),
            pltpu.VMEM(block, bf16),
            pltpu.VMEM(block, bf16),
            pltpu.VMEM(block, bf16),
            pltpu.VMEM(block, bf16),
            pltpu.VMEM(block, bf16),
            pltpu.VMEM((n_freq, 2 * loads, rows), bf16),
            pltpu.VMEM((n_freq, 2 * loads, rows), bf16),
            pltpu.VMEM((wide, rows), bf16),
            pltpu.VMEM((2, wide, rows), bf16),
            pltpu.VMEM((wide, rows), jnp.float32),
            pltpu.VMEM(block, bf16),
            pltpu.VMEM((n_freq, 2 * loads, rows), bf16),
            pltpu.SemaphoreType.DMA((5,)),
            pltpu.SemaphoreType.DMA((n_freq,)),
            pltpu.SemaphoreType.DMA((n_freq,)),
            pltpu.SemaphoreType.DMA((3,)),
            pltpu.SemaphoreType.DMA((2,)),
            pltpu.SemaphoreType.DMA((n_freq,)),
            pltpu.SemaphoreType.DMA((n_freq,)),
            pltpu.SemaphoreType.DMA((2,)),
        ],
        compiler_params=pltpu.CompilerParams(collective_id=0, has_side_effects=True),
    )(time_samples, table, inverse_offset, coupling_near, coupling_far)


def solution(mesh):
    placed = (
        P(None, "freq", "unk"),
        P(None, "freq", "unk", None),
        P(None, "freq", "unk", None),
        P(None, "freq", "unk", None),
    )
    return jax.shard_map(
        functools.partial(per_device, mesh.shape["freq"], mesh.shape["unk"]),
        mesh=mesh,
        in_specs=placed,
        out_specs=P(None, "freq", None, "unk"),
        check_vma=False,
    )
```

```python
import functools
import math

import jax
import jax.numpy as jnp
import numpy as np
from jax import lax
from jax.experimental import pallas as pl
from jax.experimental.pallas import tpu as pltpu
from jax.sharding import PartitionSpec as P

MESH = pl.DeviceIdType.MESH


def transform_matrix(times, freqs, loads):
    moment = np.arange(times)
    angle = (np.arange(freqs)[:, None] * moment[None, :] % times) * (2.0 * math.pi / times)
    damping = np.power(0.5, moment / times) / math.sqrt(times)
    table = np.stack([damping * np.cos(angle), -damping * np.sin(angle)], axis=1)
    full = np.einsum("kct,lm->kcltm", table, np.eye(loads)).astype(np.float32)
    full = full.reshape(freqs * 2 * loads, times * loads)
    high = full.astype(jnp.bfloat16)
    rest = (full - high.astype(np.float32)).astype(jnp.bfloat16)
    return np.concatenate([high, rest], axis=1)


def dot(left, right):
    return jnp.dot(left, right, preferred_element_type=jnp.float32)


def widened(value):
    half = value.shape[0] // 2
    real, imag = value[:half], value[half:]
    return jnp.concatenate(
        [jnp.concatenate([real, -imag], axis=1), jnp.concatenate([imag, real], axis=1)], axis=0
    )


def kernel(
    n_freq, n_unk, chunk,
    ts_hbm, w_hbm, o_hbm, c_hbm, f_hbm, out_ref,
    ts, w, o, c, f, near, far, sp, rb, xb, xin, acc, first_o, first_rb,
    load_sem, send_sem, recv_sem, xsend_sem, xrecv_sem, first_send_sem, first_recv_sem, share_sem,
):
    me = lax.axis_index("freq")
    pos = lax.axis_index("unk")
    loads = ts.shape[1]
    rows = o.shape[1]

    copies = [
        pltpu.make_async_copy(src, dst, load_sem.at[i])
        for i, (src, dst) in enumerate(
            [(ts_hbm, ts), (w_hbm, w), (o_hbm.at[:, 0], o), (c_hbm.at[:, 0], c), (f_hbm.at[:, 0], f)]
        )
    ]
    for copy in copies[:2]:
        copy.start()

    barrier = pltpu.get_barrier_semaphore()
    for d in range(1, n_freq):
        pl.semaphore_signal(
            barrier, inc=1, device_id={"freq": lax.rem(me + d, n_freq)}, device_id_type=MESH
        )
    for d in (1, 2):
        @pl.when(pos + d < n_unk)
        def _():
            pl.semaphore_signal(barrier, inc=1, device_id={"unk": pos + d}, device_id_type=MESH)

        @pl.when(pos >= d)
        def _():
            pl.semaphore_signal(barrier, inc=1, device_id={"unk": pos - d}, device_id_type=MESH)

    @pl.when(pos == 1)
    def _():
        for d in range(1, n_freq):
            pl.semaphore_signal(
                barrier, inc=1,
                device_id={"freq": lax.rem(me + d, n_freq), "unk": 0}, device_id_type=MESH,
            )

    for copy in copies[2:]:
        copy.start()

    copies[0].wait()
    copies[1].wait()
    samples = ts[...].astype(jnp.float32).reshape(-1, rows).astype(jnp.bfloat16)
    spectra = dot(w[...], jnp.concatenate([samples, samples], axis=0))
    sp[...] = spectra.reshape(sp.shape).astype(jnp.bfloat16)

    def reduce_block(src, dst):
        def part(i):
            at = pl.ds(pl.multiple_of(i * chunk, chunk), chunk)
            real, imag = src[0, at, :], src[1, at, :]
            weights = o[...].reshape(2 * rows, rows)
            new_real = dot(jnp.concatenate([real, -imag], axis=1), weights)
            dst[0, at, :] = (real.astype(jnp.float32) + new_real).astype(jnp.bfloat16)
            new_imag = dot(jnp.concatenate([imag, real], axis=1), weights)
            dst[1, at, :] = (imag.astype(jnp.float32) + new_imag).astype(jnp.bfloat16)

        pl.loop(0, rows // chunk)(part)

    pl.semaphore_wait(
        barrier,
        (n_freq - 1) * (1 + (pos == 0).astype(jnp.int32))
        + sum(
            (pos + d < n_unk).astype(jnp.int32) + (pos >= d).astype(jnp.int32) for d in (1, 2)
        ),
    )

    def share_offset():
        return pltpu.make_async_remote_copy(
            src_ref=o_hbm.at[:, 0], dst_ref=first_o,
            send_sem=share_sem.at[0], recv_sem=share_sem.at[1],
            device_id={"unk": 1}, device_id_type=MESH,
        )

    def share_spectra(target, source, at):
        return pltpu.make_async_remote_copy(
            src_ref=sp.at[target], dst_ref=first_rb.at[source],
            send_sem=first_send_sem.at[at], recv_sem=first_recv_sem.at[source],
            device_id={"freq": target, "unk": 1}, device_id_type=MESH,
        )

    def other(d):
        upper = (me * 2) // n_freq
        rising = (d - 1) + (d - 1 >= me).astype(jnp.int32)
        falling = (n_freq - d) - (n_freq - d <= me).astype(jnp.int32)
        return upper * rising + (1 - upper) * falling

    @pl.when(pos == 0)
    def _():
        for d in range(1, n_freq):
            share_spectra(other(d), me, d).start()
        share_spectra(me, me, 0).start()
        share_offset().start()

    sends = []
    for d in range(1, n_freq):
        target = other(d)
        send = pltpu.make_async_remote_copy(
            src_ref=sp.at[target], dst_ref=rb.at[me],
            send_sem=send_sem.at[d], recv_sem=recv_sem.at[me],
            device_id={"freq": target}, device_id_type=MESH,
        )
        send.start()
        sends.append(send)
    rb[me] = sp[me]

    copies[2].wait()
    copies[3].wait()
    copies[4].wait()

    @pl.when(pos >= 1)
    def _():
        reduce_block(c, near)

    @pl.when(pos >= 2)
    def _():
        reduce_block(f, far)

    for d in range(1, n_freq):
        source = lax.rem(me + n_freq - d, n_freq)
        pltpu.make_async_remote_copy(
            src_ref=rb.at[source], dst_ref=rb.at[source],
            send_sem=send_sem.at[d], recv_sem=recv_sem.at[source],
            device_id={"freq": source}, device_id_type=MESH,
        ).wait_recv()

    odd = lax.rem(pos, 2) == 1
    ahead = lax.rem(pos + 1, n_unk)

    def to_next(slot, src, sem):
        return pltpu.make_async_remote_copy(
            src_ref=src, dst_ref=xin.at[slot],
            send_sem=xsend_sem.at[sem], recv_sem=xrecv_sem.at[slot],
            device_id={"unk": ahead}, device_id_type=MESH,
        )

    def to_second():
        return pltpu.make_async_remote_copy(
            src_ref=xb, dst_ref=xin.at[1],
            send_sem=xsend_sem.at[1], recv_sem=xrecv_sem.at[1],
            device_id={"unk": lax.rem(pos + 2, n_unk)}, device_id_type=MESH,
        )

    def drive(spectra_in, offset):
        got = spectra_in[...].astype(jnp.float32)
        got = jnp.concatenate(
            [got[:, :loads].reshape(-1, rows), got[:, loads:].reshape(-1, rows)], axis=0
        )
        return got + dot(widened(got.astype(jnp.bfloat16)), offset[...].reshape(2 * rows, rows))

    acc[...] = drive(rb, o)

    @pl.when(pos == 1)
    def _():
        for d in range(n_freq):
            source = lax.rem(me + n_freq - d, n_freq)
            share_spectra(source, source, d).wait_recv()
        share_offset().wait_recv()
        first = drive(first_rb, first_o).astype(jnp.bfloat16)
        xin[0] = first

        @pl.when(pos + 1 < n_unk)
        def _():
            to_next(1, xin.at[0], 2).start()

        acc[...] -= dot(widened(first), near[...].reshape(2 * rows, rows))


    has_next = jnp.logical_and(pos >= 1, pos + 1 < n_unk)
    has_second = jnp.logical_and(jnp.logical_and(pos >= 2, pos + 2 < n_unk), jnp.logical_not(odd))
    hands_on = jnp.logical_and(jnp.logical_and(pos >= 2, has_next), jnp.logical_not(odd))

    @pl.when(pos >= 2)
    def _():
        @pl.when(jnp.logical_not(odd))
        def _():
            to_second().wait_recv()

        @pl.when(odd)
        def _():
            to_next(1, xin.at[0], 2).wait_recv()

        acc[...] -= dot(widened(xin[1]), far[...].reshape(2 * rows, rows))

    @pl.when(pos >= 2)
    def _():
        to_next(0, xb, 0).wait_recv()

        @pl.when(hands_on)
        def _():
            to_next(1, xin.at[0], 2).start()

        acc[...] -= dot(widened(xin[0]), near[...].reshape(2 * rows, rows))

    solved = acc[...].astype(jnp.bfloat16)
    xb[...] = solved
    out_ref[...] = solved.reshape(out_ref.shape)

    @pl.when(has_next)
    def _():
        to_next(0, xb, 0).start()

    @pl.when(has_second)
    def _():
        to_second().start()


    for send in sends:
        send.wait_send()

    @pl.when(pos == 0)
    def _():
        for d in range(n_freq):
            share_spectra(me, me, d).wait_send()
        share_offset().wait_send()

    @pl.when(jnp.logical_or(hands_on, jnp.logical_and(pos == 1, has_next)))
    def _():
        to_next(1, xin.at[0], 2).wait_send()

    @pl.when(has_next)
    def _():
        to_next(0, xb, 0).wait_send()

    @pl.when(has_second)
    def _():
        to_second().wait_send()


def per_device(n_freq, n_unk, time_samples, inverse_offset, coupling_near, coupling_far):
    times, loads, rows = time_samples.shape
    freqs = inverse_offset.shape[1] * n_freq
    table = jnp.asarray(transform_matrix(times, freqs, loads))
    block = (2, rows, rows)
    wide = 2 * n_freq * loads
    bf16 = jnp.bfloat16
    return pl.pallas_call(
        functools.partial(kernel, n_freq, n_unk, min(256, rows)),
        out_shape=pltpu.VMEM((2, 1, n_freq * loads, rows), bf16),
        in_specs=[pl.BlockSpec(memory_space=pl.ANY)] * 5,
        out_specs=pl.BlockSpec(memory_space=pltpu.VMEM),
        scratch_shapes=[
            pltpu.VMEM(time_samples.shape, bf16),
            pltpu.VMEM(table.shape, bf16),
            pltpu.VMEM(block, bf16),
            pltpu.VMEM(block, bf16),
            pltpu.VMEM(block, bf16),
            pltpu.VMEM(block, bf16),
            pltpu.VMEM(block, bf16),
            pltpu.VMEM((n_freq, 2 * loads, rows), bf16),
            pltpu.VMEM((n_freq, 2 * loads, rows), bf16),
            pltpu.VMEM((wide, rows), bf16),
            pltpu.VMEM((2, wide, rows), bf16),
            pltpu.VMEM((wide, rows), jnp.float32),
            pltpu.VMEM(block, bf16),
            pltpu.VMEM((n_freq, 2 * loads, rows), bf16),
            pltpu.SemaphoreType.DMA((5,)),
            pltpu.SemaphoreType.DMA((n_freq,)),
            pltpu.SemaphoreType.DMA((n_freq,)),
            pltpu.SemaphoreType.DMA((3,)),
            pltpu.SemaphoreType.DMA((2,)),
            pltpu.SemaphoreType.DMA((n_freq,)),
            pltpu.SemaphoreType.DMA((n_freq,)),
            pltpu.SemaphoreType.DMA((2,)),
        ],
        compiler_params=pltpu.CompilerParams(collective_id=0, has_side_effects=True),
    )(time_samples, table, inverse_offset, coupling_near, coupling_far)


def solution(mesh):
    placed = (
        P(None, "freq", "unk"),
        P(None, "freq", "unk", None),
        P(None, "freq", "unk", None),
        P(None, "freq", "unk", None),
    )
    return jax.shard_map(
        functools.partial(per_device, mesh.shape["freq"], mesh.shape["unk"]),
        mesh=mesh,
        in_specs=placed,
        out_specs=P(None, "freq", None, "unk"),
        check_vma=False,
    )
```
